1024 devices in a mesh: gx: 32 (over x, y), gy: 32 (over z, core).
Axes of the slice: x: 4, y: 8, z: 16, core: 2. Of those that a mesh axis runs over, the one named last changes fastest.
Arguments:
- basis: float32 [32, 512, 256, 128], P(None, 'gx', 'gy'), may hold values from -21 to 21
- classes: int32 [512, 256, 128], P('gx', 'gy'), may hold values from 0 to 7
- ports: int32 [512, 256, 128], P('gx', 'gy'), may hold values from 0 to 8, as said below
- taps: float32 [8, 42], replicated, may hold values from 0.05 to 0.5
- port_gain: float32 [8], replicated, may hold values from 0.5 to 4
Outputs:
- next_block: float32 [8, 512, 256, 128], P(None, 'gx', 'gy')
- projection: float32 [32, 8], replicated
- triangle: float32 [8, 8], replicated
The draws below stay inside these ranges and needn't reach their ends.
Inputs may be any that keep to these rules, and one draw needn't show every extreme that they name: `ports`: 0 means the cell belongs to no port; p in 1..8 names port p.
All inputs are finite; a program needn't handle non-finite values.
Results may differ from the reference program's by a relative error of at most 0.00029.
Values sent between devices are 32-bit elements; how exact they have to be, the bound alone decides.
No kernel may reach another device: no remote copies, remote signals or barrier semaphores. Data moves between devices by JAX's collectives and lax.ppermute only.
A program may use at most 32 MiB of HBM per device.

```python
import math
import jax
import jax.numpy as jnp
from jax import lax

COLS = 8
BLOCKS = 4
REACH = 7
MAT = 8
PORTS = 8
NX = 512
NY = 256
NZ = 128


def draw_basis(key, part):
    first, second = jax.random.split(key)
    shape = (BLOCKS * COLS, NX, NY, NZ)
    values = jnp.clip(jax.random.normal(first, shape, jnp.float32), -6.0, 6.0)
    spread = jax.random.uniform(second, (1, NX, NY, NZ), jnp.float32)
    cell_scale = jnp.power(10.0, spread) / 4.6365
    position = jnp.arange(NX, dtype=jnp.float32) / NX
    ramp = jnp.power(3.0, position) / 1.9082
    return values * cell_scale * ramp[None, :, None, None]


def draw_ports(key, part):
    first, second = jax.random.split(jax.random.fold_in(key, 17))
    chosen = jax.random.randint(first, (NX, NY, NZ), 0, 4)
    which = jax.random.randint(second, (NX, NY, NZ), 1, PORTS + 1)
    return jnp.where(chosen == 0, which, 0).astype(jnp.int32)


def place_ends(array, own_key, smallest, top_value):
    spot = [jax.random.randint(jax.random.fold_in(own_key, axis), (), 0, length) for axis, length in enumerate(array.shape)]
    widest = array.shape.index(max(array.shape))
    beside = spot[:widest] + [(spot[widest] + 1) % array.shape[widest]] + spot[widest + 1:]
    return array.at[tuple(spot)].set(smallest).at[tuple(beside)].set(top_value)


def setup_inputs(seed: int = 0) -> dict:
    splits = jax.random.split(jax.random.key(seed), 6)
    basis = draw_basis(jax.random.fold_in(splits[5], 71), 0)
    classes = place_ends(jax.random.randint(splits[1], (NX, NY, NZ), 0, MAT), jax.random.fold_in(splits[1], 1), 0, MAT - 1).astype(jnp.int32)
    ports = draw_ports(jax.random.fold_in(splits[5], 71), 0)
    taps = jnp.clip(jnp.exp(jax.random.uniform(splits[3], (MAT, 6 * REACH), jnp.float32, math.log(0.05), math.log(0.5))), 0.05, 0.5)
    port_gain = jnp.clip(jnp.exp(jax.random.uniform(splits[4], (PORTS,), jnp.float32, math.log(0.5), math.log(4.0))), 0.5, 4.0)
    return dict(basis=basis, classes=classes, ports=ports, taps=taps, port_gain=port_gain)


def reference(basis, classes, ports, taps, port_gain):
    highest = lax.Precision.HIGHEST
    gains_full = jnp.concatenate([jnp.zeros((1,), jnp.float32), port_gain])
    diag = 1.0 + jnp.sum(taps, axis=1)[classes] + gains_full[ports]
    block = basis[(BLOCKS - 1) * COLS:]
    sizes_all = (NX, NY, NZ)

    def apply_column(column):
        result = diag * column
        for dim in range(3):
            widths = [(0, 0), (0, 0), (0, 0)]
            widths[dim] = (REACH, REACH)
            padded = jnp.pad(column, widths)
            for j in range(2 * REACH):
                offset = j - REACH if j < REACH else j - REACH + 1
                shifted = lax.slice_in_dim(padded, REACH + offset, REACH + offset + sizes_all[dim], axis=dim)
                result = result - taps[:, 2 * REACH * dim + j][classes] * shifted
        return result
    image = lax.map(apply_column, block)
    cells = NX * NY * NZ
    basis_flat = basis.reshape(BLOCKS * COLS, cells)
    image_flat = image.reshape(COLS, cells)
    projection = jnp.dot(basis_flat, image_flat.T, precision=highest) / cells
    remainder = image_flat - jnp.dot(projection.T, basis_flat, precision=highest)
    gram = jnp.dot(remainder, remainder.T, precision=highest) / cells
    lower = jnp.linalg.cholesky(gram)
    solved = lax.linalg.triangular_solve(lower, remainder, left_side=True, lower=True)
    return (solved.reshape(COLS, NX, NY, NZ), projection, lower.T)
```

```python
import functools

import jax
import jax.numpy as jnp
from jax import lax
from jax.experimental import pallas as pl
from jax.experimental.pallas import tpu as pltpu
from jax.sharding import Mesh
from jax.sharding import PartitionSpec as P

COLS = 8
BLOCKS = 4
REACH = 7
MAT = 8
PORTS = 8
AXES = ("gx_0", "gx_1", "gy_0", "gy_1")
GX = ("gx_0", "gx_1")
GY = ("gy_0", "gy_1")
SUB = 8
LANES = 128
HIGHEST = lax.Precision.HIGHEST
F32 = jnp.float32
BF16 = jnp.bfloat16
VMEM = pl.BlockSpec(memory_space=pltpu.VMEM)
HBM = pl.BlockSpec(memory_space=pltpu.MemorySpace.HBM)

QQ_AT = (0, 8, 24, 48)
QW_AT = 80
WW_AT = 112


def in_hbm(value):
    return pltpu.with_memory_space_constraint(value, pltpu.MemorySpace.HBM)


def limit(mebibytes):
    return pltpu.CompilerParams(vmem_limit_bytes=mebibytes * 2**20)


def offset_of(j):
    return j - REACH if j < REACH else j - REACH + 1


def index_of(k):
    return k + REACH if k < 0 else k + REACH - 1


def iota(shape, dim):
    return lax.broadcasted_iota(jnp.int32, shape, dim)


def split(value):
    high = value.astype(BF16)
    return high, (value - high.astype(F32)).astype(BF16)


def rows_dot(a, b, precision=None):
    return lax.dot_general(
        a, b, (((1,), (1,)), ((), ())), precision=precision, preferred_element_type=F32
    )


def plain_dot(a, b, precision=None):
    return lax.dot_general(
        a, b, (((1,), (0,)), ((), ())), precision=precision, preferred_element_type=F32
    )


def shift_of(totals):
    return jnp.mean(totals, axis=0, keepdims=True)


def wide_lanes(value, room):
    room[...] = jnp.zeros(room.shape, F32)
    room[:, : value.shape[1]] = value
    return room[...]


def odd_place(axes):
    place = 0
    for axis in axes:
        place = place * lax.axis_size(axis) + lax.axis_index(axis)
    return lax.rem(place, 2)


def edges_kernel(basis_ref, block_ref, xa_ref, xb_ref, sems):
    odd = odd_place(GX)
    block = basis_ref.at[(BLOCKS - 1) * COLS : BLOCKS * COLS]
    far = basis_ref.shape[1] - REACH
    jobs = (
        (block, block_ref),
        (block.at[:, pl.ds((1 - odd) * far, REACH)], xa_ref),
        (block.at[:, pl.ds(odd * far, REACH)], xb_ref),
    )
    copies = [pltpu.make_async_copy(*job, sems.at[i]) for i, job in enumerate(jobs)]
    for copy in copies:
        copy.start()
    for copy in copies:
        copy.wait()


def local_kernel(taps_ref, gain_ref, basis_ref, block_ref, classes_hbm, ports_hbm,
                 part_ref, coef_x_ref, coef_y_ref, both_ref, sums_ref,
                 along_x, along_y, gains, room, spread, coefs, whole, classes_ref, ports_ref, sems):
    size_x = classes_ref.shape[0]
    jobs = ((classes_hbm, classes_ref), (ports_hbm, ports_ref), (basis_ref, whole))
    *loads, load = [pltpu.make_async_copy(*job, sems.at[i]) for i, job in enumerate(jobs)]
    for copy in (*loads, load):
        copy.start()
    row = iota((SUB, LANES), 0)
    lane = iota((SUB, LANES), 1)
    taps = wide_lanes(taps_ref[...], room)
    totals = jnp.broadcast_to(jnp.sum(taps, axis=1, keepdims=True), (MAT, LANES))
    taps = jnp.where(lane == 6 * REACH, totals - shift_of(totals), taps)
    high, rest = split(taps)
    middle, low = split((taps - high.astype(F32)))
    each = jnp.concatenate([high.astype(F32), middle.astype(F32), low.astype(F32)], axis=0)
    each = jnp.broadcast_to(each[:, None, :], (3 * MAT, SUB, LANES)).reshape(3 * MAT * SUB, LANES)
    count = 6 * REACH + 1
    chosen = (iota((count * SUB, LANES), 0) // SUB == iota((count * SUB, LANES), 1)).astype(BF16)
    by_kind = rows_dot(chosen, each.astype(BF16))
    same = (iota(by_kind.shape, 0) % SUB) == (iota(by_kind.shape, 1) % SUB)
    spread[...] = jnp.where(same, by_kind, 0.0).astype(BF16)
    gain = wide_lanes(jnp.broadcast_to(gain_ref[...], (SUB, PORTS)), room)
    for p in range(PORTS):
        gains[p] = jnp.broadcast_to(gain[:, p : p + 1], (SUB, LANES))
    zero = jnp.zeros((SUB, LANES), F32)
    for x in range(REACH):
        for c in range(COLS):
            along_x[x, c] = zero
            along_x[REACH + size_x + x, c] = zero

    def prepare(x, carry):
        for c in range(COLS):
            v = block_ref[c, x]
            along_x[REACH + x, c] = v
            along_y[x, c, 0:SUB] = v
            along_y[x, c, SUB : 2 * SUB] = v
        return carry

    lax.fori_loop(0, size_x, prepare, 0)
    for copy in loads:
        copy.wait()

    def hot(x):
        kind = classes_ref[x]
        one = jnp.concatenate([(kind == m).astype(F32) for m in range(MAT)], axis=0).astype(BF16)
        return jnp.concatenate([one, one, one], axis=0)

    def plane(x, at):
        port = ports_ref[x]
        coef_at = lambda t: coefs[t * SUB : (t + 1) * SUB, at * LANES : (at + 1) * LANES]
        own = [along_x[REACH + x, c] for c in range(COLS)]
        diag = coef_at(6 * REACH)
        extra = zero
        for p in range(PORTS):
            extra = jnp.where(port == p + 1, gains[p], extra)
        diag = diag + extra
        acc = [diag * v for v in own]
        for j in range(2 * REACH):
            coef = coef_at(j)
            for c in range(COLS):
                acc[c] = acc[c] - coef * along_x[REACH + x + offset_of(j), c]
        for j in range(REACH):
            coef_x_ref[x, j] = jnp.where(x < size_x // 2, coef_at(j), coef_at(REACH + j))
        for k in range(1, REACH + 1):
            up = coef_at(2 * REACH + index_of(k))
            down = coef_at(2 * REACH + index_of(k - SUB))
            inside = row < SUB - k
            coef = jnp.where(inside, up, down)
            coef_y_ref[x, k - 1] = jnp.where(inside, down, up)
            for c in range(COLS):
                acc[c] = acc[c] - coef * along_y[x, c, k : k + SUB]
        for j in range(2 * REACH):
            k = offset_of(j)
            coef = jnp.where((lane + k >= 0) & (lane + k < LANES), coef_at(4 * REACH + j), 0.0)
            for c in range(COLS):
                acc[c] = acc[c] - coef * pltpu.roll(own[c], (-k) % LANES, 1)
        for c in range(COLS):
            part_ref[x, c] = acc[c]

    def pair(i, carry):
        coefs[...] = plain_dot(spread[...], jnp.concatenate([hot(2 * i), hot(2 * i + 1)], axis=1))
        plane(2 * i, 0)
        plane(2 * i + 1, 1)
        return carry

    lax.fori_loop(0, size_x // 2, pair, 0)

    load.wait()
    wide = BLOCKS * COLS
    lines = size_x * SUB

    def store(x, carry):
        for y in range(SUB):
            high, low = split(whole[pl.ds(x * SUB + y, wide, stride=lines), :])
            at = pl.ds(pl.multiple_of((x * SUB + y) * LANES, LANES), LANES)
            both_ref[:, at] = jnp.concatenate([high, low], axis=0)
        return carry

    lax.fori_loop(0, size_x, store, 0)
    both = both_ref[...]
    products = rows_dot(both, both)
    products = jnp.concatenate([products, jnp.zeros((2 * wide, LANES - 2 * wide), F32)], axis=1)
    products = products[:wide] + products[wide:]
    products = products + pltpu.roll(products, LANES - wide, 1)
    sums = zero
    for a in range(BLOCKS):
        block = jnp.where(lane < (a + 1) * COLS, products[a * COLS : (a + 1) * COLS], 0.0)
        sums = sums + (pltpu.roll(block, QQ_AT[a], 1) if QQ_AT[a] else block)
    sums_ref[...] = sums


def halo_kernel(part_ref, coef_x_ref, coef_y_ref, both_ref, sums_ref,
                xa_ref, xb_ref, ya_ref, yb_ref,
                w_ref, out_ref, around, image, room):
    size_x = part_ref.shape[0]
    odd_x = odd_place(GX) == 1
    odd_y = odd_place(GY)
    below_x = lambda p, c: jnp.where(odd_x, xa_ref[c, p], xb_ref[c, p])
    above_x = lambda p, c: jnp.where(odd_x, xb_ref[c, p], xa_ref[c, p])
    at_a = pl.ds(pl.multiple_of((1 - odd_y) * SUB, SUB), SUB)
    at_b = pl.ds(pl.multiple_of(odd_y * SUB, SUB), SUB)
    lines = size_x * SUB
    for x in range(size_x):
        for c in range(COLS):
            around[x, c, at_a] = ya_ref[c, x]
            around[x, c, at_b] = yb_ref[c, x]
        acc = [part_ref[x, c] for c in range(COLS)]
        for k in range(1, REACH + 1):
            coef = coef_y_ref[x, k - 1]
            for c in range(COLS):
                acc[c] = acc[c] - coef * around[x, c, k : k + SUB]
        for j in range(2 * REACH):
            at = x + offset_of(j)
            if 0 <= at < size_x:
                continue
            coef = coef_x_ref[x, j % REACH]
            for c in range(COLS):
                value = below_x(at + REACH, c) if at < 0 else above_x(at - size_x, c)
                acc[c] = acc[c] - coef * value
        for c in range(COLS):
            image[c * lines + x * SUB : c * lines + (x + 1) * SUB, :] = acc[c]
        for y in range(SUB):
            high, low = split(image[pl.ds(x * SUB + y, COLS, stride=lines), :])
            at = (x * SUB + y) * LANES
            w_ref[:, at : at + LANES] = jnp.concatenate([high, low], axis=0)
    w = w_ref[...]
    wide = BLOCKS * COLS
    lane = iota((SUB, LANES), 1)
    q_w = wide_lanes(rows_dot(w, both_ref[...]), room)
    q_w = q_w[:COLS] + q_w[COLS:]
    q_w = jnp.where(lane < wide, q_w + pltpu.roll(q_w, LANES - wide, 1), 0.0)
    w_w = wide_lanes(rows_dot(w, w), room)
    w_w = w_w[:COLS] + w_w[COLS:]
    w_w = jnp.where(lane < COLS, w_w + pltpu.roll(w_w, LANES - COLS, 1), 0.0)
    out_ref[...] = sums_ref[...] + pltpu.roll(q_w, QW_AT, 1) + pltpu.roll(w_w, WW_AT, 1)


def fold_kernel(*refs):
    *tiles, out_ref = refs
    total = sum(jnp.sum(tile[...], axis=0) if tile.ndim == 3 else tile[...] for tile in tiles)
    out_ref[...] = jnp.broadcast_to(total[None], out_ref.shape)


def root_inverse(value):
    guess = lax.rsqrt(value)
    return guess * (1.5 - 0.5 * value * guess * guess)


def finish_kernel(scale, taps_ref, received_ref, both_ref, w_ref,
                  next_ref, projection_ref, triangle_ref, room, result, sems):
    size_x = next_ref.shape[1] // SUB
    wide = BLOCKS * COLS
    row = iota((SUB, LANES), 0)
    lane = iota((SUB, LANES), 1)
    sums = jnp.sum(received_ref[...], axis=0) * scale
    taps = wide_lanes(taps_ref[...], room)
    totals = jnp.broadcast_to(jnp.sum(taps, axis=1, keepdims=True), (MAT, LANES))
    shift = 1.0 + shift_of(totals)
    part_t = jnp.where(lane < wide, pltpu.roll(sums, LANES - QW_AT, 1), 0.0)
    w_w = jnp.where(lane < COLS, pltpu.roll(sums, LANES - WW_AT, 1), 0.0)
    blocks = []
    for a in range(BLOCKS):
        block = pltpu.roll(sums, LANES - QQ_AT[a], 1) if QQ_AT[a] else sums
        block = jnp.where(lane < (a + 1) * COLS, block, 0.0)
        last = block
        blocks.append(jnp.where(lane >= a * COLS, 0.5 * block, block))
    unit = jnp.where(lane == row + (wide - COLS), 1.0, 0.0)
    p_t = part_t + shift * last
    back_t = shift * (unit - last) - part_t
    lower = jnp.concatenate(blocks + [jnp.zeros((LANES - wide, LANES), F32)], axis=0)
    rest = jnp.zeros((LANES - SUB, LANES), F32)
    inner = part_t + plain_dot(back_t, lower, HIGHEST)
    gram = (
        w_w
        + rows_dot(inner, jnp.concatenate([back_t, rest], axis=0), HIGHEST)
        + rows_dot(back_t, jnp.concatenate([inner, rest], axis=0), HIGHEST)
    )
    apply = jnp.where(lane == row + wide, 1.0, back_t)
    for k in range(COLS):
        column = jnp.broadcast_to(gram[:, k : k + 1], (SUB, LANES))
        pivot = jnp.broadcast_to(gram[k : k + 1, k : k + 1], (SUB, LANES))
        inverse = root_inverse(pivot)
        gram_row = jnp.broadcast_to(gram[k : k + 1, :], (SUB, LANES)) * inverse
        apply_row = jnp.broadcast_to(apply[k : k + 1, :], (SUB, LANES)) * inverse
        factor = jnp.where(row > k, column * inverse, 0.0)
        gram = jnp.where(row == k, gram_row, gram - factor * gram_row)
        apply = jnp.where(row == k, apply_row, apply - factor * apply_row)
    triangle_ref[...] = jnp.where(lane >= row, gram, 0.0)[:, :COLS]
    projection_ref[...] = p_t[:, :wide]
    high, low = split(apply)
    pieces = jnp.concatenate([high.astype(F32), low.astype(F32)], axis=0)
    lane = iota(pieces.shape, 1)
    on_both = jnp.where(lane < wide, pieces, pltpu.roll(pieces, wide, 1))[:, : 2 * wide].astype(BF16)
    pieces = pltpu.roll(pieces, LANES - wide, 1)
    on_w = jnp.where(lane < COLS, pieces, pltpu.roll(pieces, COLS, 1))[:, : 2 * COLS].astype(BF16)
    lines = size_x * SUB
    group = size_x // 4
    copies = []
    for x in range(size_x):
        at = slice(x * SUB * LANES, (x + 1) * SUB * LANES)
        block = plain_dot(on_both, both_ref[:, at]) + plain_dot(on_w, w_ref[:, at])
        block = block[:COLS] + block[COLS:]
        for y in range(SUB):
            result[pl.ds(x * SUB + y, COLS, stride=lines), :] = block[:, y * LANES : (y + 1) * LANES]
        if x % group == group - 1:
            for c in range(COLS):
                copies.append(pltpu.make_async_copy(
                    result.at[pl.ds(c * lines + (x + 1 - group) * SUB, group * SUB)],
                    next_ref.at[c, pl.ds((x + 1 - group) * SUB, group * SUB)],
                    sems.at[x // group, c],
                ))
                copies[-1].start()
    for copy in copies:
        copy.wait()


def swaps(devices):
    first = [(i, i ^ 1) for i in range(devices)]
    second = [pair for i in range(1, devices - 1, 2) for pair in ((i, i + 1), (i + 1, i))]
    return first, second


def per_device(basis, classes, ports, taps, port_gain):
    size_x, size_y, size_z = classes.shape
    x_first, x_second = swaps(lax.axis_size(GX))
    y_first, y_second = swaps(lax.axis_size(GY))
    shape = jax.ShapeDtypeStruct
    wide, cells, lines = BLOCKS * COLS, size_x * size_y * size_z, size_x * SUB
    tile = shape((SUB, LANES), F32)
    edge = shape((COLS, REACH, SUB, LANES), F32)
    block, xa, xb = pl.pallas_call(
        edges_kernel,
        out_shape=(shape((COLS, size_x, SUB, LANES), F32), edge, edge),
        in_specs=[HBM],
        out_specs=(VMEM,) * 3,
        scratch_shapes=[pltpu.SemaphoreType.DMA((3,))],
        compiler_params=limit(4),
        name="edges",
    )(in_hbm(basis))
    yb = lax.ppermute(block, GY, y_second)
    xb = lax.ppermute(xb, GX, x_second)
    xa = lax.ppermute(xa, GX, x_first)
    ya = lax.ppermute(block, GY, y_first)
    part, coef_x, coef_y, both, sums = pl.pallas_call(
        local_kernel,
        out_shape=(
            shape((size_x, COLS, SUB, LANES), F32),
            shape((size_x, REACH, SUB, LANES), F32),
            shape((size_x, REACH, SUB, LANES), F32),
            shape((2 * wide, cells), BF16),
            tile,
        ),
        in_specs=[VMEM, VMEM, HBM, VMEM, HBM, HBM],
        out_specs=(VMEM,) * 5,
        scratch_shapes=[
            pltpu.VMEM((size_x + 2 * REACH, COLS, SUB, LANES), F32),
            pltpu.VMEM((size_x, COLS, 2 * SUB, LANES), F32),
            pltpu.VMEM((PORTS, SUB, LANES), F32),
            pltpu.VMEM((SUB, LANES), F32),
            pltpu.VMEM(((6 * REACH + 1) * SUB, 3 * MAT * SUB), BF16),
            pltpu.VMEM(((6 * REACH + 1) * SUB, 2 * LANES), F32),
            pltpu.VMEM((wide * lines, LANES), F32),
            pltpu.VMEM((size_x, SUB, LANES), jnp.int32),
            pltpu.VMEM((size_x, SUB, LANES), jnp.int32),
            pltpu.SemaphoreType.DMA((3,)),
        ],
        compiler_params=limit(16),
        cost_estimate=pl.CostEstimate(flops=10**9, bytes_accessed=8 * 2**20, transcendentals=0),
        name="local",
    )(taps, port_gain[None], in_hbm(basis.reshape(wide * lines, LANES)), block, in_hbm(classes), in_hbm(ports))
    w, sums = pl.pallas_call(
        halo_kernel,
        out_shape=(shape((2 * COLS, cells), BF16), tile),
        in_specs=[VMEM] * 9,
        out_specs=(VMEM,) * 2,
        scratch_shapes=[
            pltpu.VMEM((size_x, COLS, 2 * SUB, LANES), F32),
            pltpu.VMEM((COLS * lines, LANES), F32),
            pltpu.VMEM((2 * COLS, LANES), F32),
        ],
        compiler_params=limit(8),
        name="halo",
    )(part, coef_x, coef_y, both, sums, xa, xb, ya, yb)

    def fold(copies, *tiles):
        return pl.pallas_call(
            fold_kernel,
            out_shape=shape((copies, SUB, LANES), F32),
            in_specs=[VMEM] * len(tiles),
            out_specs=VMEM,
            compiler_params=limit(2),
            name="fold",
        )(*tiles)

    beside = lax.ppermute(sums, "gy_1", [(0, 1), (1, 0)])
    along_gx = lax.all_to_all(fold(lax.axis_size(GX), sums, beside), GX, 0, 0)
    received = lax.all_to_all(fold(lax.axis_size("gy_0"), along_gx), "gy_0", 0, 0)
    total = cells * lax.axis_size(GX) * lax.axis_size(GY)
    next_block, projection, triangle = pl.pallas_call(
        functools.partial(finish_kernel, 1.0 / total),
        out_shape=(
            shape((COLS, lines, LANES), F32),
            shape((COLS, wide), F32),
            shape((COLS, COLS), F32),
        ),
        in_specs=[VMEM] * 4,
        out_specs=(HBM, VMEM, VMEM),
        scratch_shapes=[
            pltpu.VMEM((MAT, LANES), F32),
            pltpu.VMEM((COLS * lines, LANES), F32),
            pltpu.SemaphoreType.DMA((4, COLS)),
        ],
        compiler_params=limit(8),
        name="finish",
    )(taps, received, both, w)
    return next_block.reshape(COLS, size_x, size_y, size_z), projection.T, triangle


def solution(mesh):
    split_mesh = Mesh(mesh.devices.reshape(4, 8, 16, 2), AXES)
    in_specs = (P(None, GX, GY, None), P(GX, GY, None), P(GX, GY, None), P(), P())
    out_specs = (P(None, GX, GY, None), P(), P())
    return jax.shard_map(
        per_device, mesh=split_mesh, in_specs=in_specs, out_specs=out_specs, check_vma=False
    )
```

```python
import functools

import jax
import jax.numpy as jnp
from jax import lax
from jax.experimental import pallas as pl
from jax.experimental.pallas import tpu as pltpu
from jax.sharding import Mesh
from jax.sharding import PartitionSpec as P

COLS = 8
BLOCKS = 4
REACH = 7
MAT = 8
PORTS = 8
AXES = ("gx_0", "gx_1", "gy_0", "gy_1")
GX = ("gx_0", "gx_1")
GY = ("gy_0", "gy_1")
SUB = 8
LANES = 128
HIGHEST = lax.Precision.HIGHEST
F32 = jnp.float32
BF16 = jnp.bfloat16
VMEM = pl.BlockSpec(memory_space=pltpu.VMEM)
HBM = pl.BlockSpec(memory_space=pltpu.MemorySpace.HBM)

QQ_AT = (0, 8, 24, 48)
QW_AT = 80
WW_AT = 112


def in_hbm(value):
    return pltpu.with_memory_space_constraint(value, pltpu.MemorySpace.HBM)


def limit(mebibytes):
    return pltpu.CompilerParams(vmem_limit_bytes=mebibytes * 2**20)


def offset_of(j):
    return j - REACH if j < REACH else j - REACH + 1


def index_of(k):
    return k + REACH if k < 0 else k + REACH - 1


def iota(shape, dim):
    return lax.broadcasted_iota(jnp.int32, shape, dim)


def split(value):
    high = value.astype(BF16)
    return high, (value - high.astype(F32)).astype(BF16)


def rows_dot(a, b, precision=None):
    return lax.dot_general(
        a, b, (((1,), (1,)), ((), ())), precision=precision, preferred_element_type=F32
    )


def plain_dot(a, b, precision=None):
    return lax.dot_general(
        a, b, (((1,), (0,)), ((), ())), precision=precision, preferred_element_type=F32
    )


def shift_of(totals):
    return jnp.mean(totals, axis=0, keepdims=True)


def wide_lanes(value, room):
    room[...] = jnp.zeros(room.shape, F32)
    room[:, : value.shape[1]] = value
    return room[...]


def odd_place(axes):
    place = 0
    for axis in axes:
        place = place * lax.axis_size(axis) + lax.axis_index(axis)
    return lax.rem(place, 2)


def edges_kernel(basis_ref, block_ref, xa_ref, xb_ref, sems):
    odd = odd_place(GX)
    block = basis_ref.at[(BLOCKS - 1) * COLS : BLOCKS * COLS]
    far = basis_ref.shape[1] - REACH
    jobs = (
        (block, block_ref),
        (block.at[:, pl.ds((1 - odd) * far, REACH)], xa_ref),
        (block.at[:, pl.ds(odd * far, REACH)], xb_ref),
    )
    copies = [pltpu.make_async_copy(*job, sems.at[i]) for i, job in enumerate(jobs)]
    for copy in copies:
        copy.start()
    for copy in copies:
        copy.wait()


def local_kernel(taps_ref, gain_ref, basis_ref, block_ref, classes_hbm, ports_hbm,
                 part_ref, coef_x_ref, coef_y_ref, both_ref, sums_ref,
                 along_x, along_y, gains, room, spread, hots, coefs, whole, own, shifts, shifted,
                 classes_ref, ports_ref, sems):
    size_x = classes_ref.shape[0]
    wide = BLOCKS * COLS
    jobs = ((classes_hbm, classes_ref), (ports_hbm, ports_ref))
    loads = [pltpu.make_async_copy(*job, sems.at[i]) for i, job in enumerate(jobs)]
    basis_loads = [pltpu.make_async_copy(basis_ref.at[c], whole.at[:, c], sems.at[2 + c]) for c in range(wide)]
    for copy in (*loads, *basis_loads):
        copy.start()
    row = iota((SUB, LANES), 0)
    lane = iota((SUB, LANES), 1)
    taps = wide_lanes(taps_ref[...], room)
    totals = jnp.broadcast_to(jnp.sum(taps, axis=1, keepdims=True), (MAT, LANES))
    taps = jnp.where(lane == 6 * REACH, totals - shift_of(totals), taps)
    high, _ = split(taps)
    middle, low = split((taps - high.astype(F32)))
    each = jnp.concatenate([high.astype(F32), middle.astype(F32), low.astype(F32)], axis=0)
    each = jnp.broadcast_to(each[:, None, :], (3 * MAT, SUB, LANES)).reshape(3 * MAT * SUB, LANES)
    count = 6 * REACH + 1
    chosen = (iota((count * SUB, LANES), 0) // SUB == iota((count * SUB, LANES), 1)).astype(BF16)
    by_kind = rows_dot(chosen, each.astype(BF16))
    same = (iota(by_kind.shape, 0) % SUB) == (iota(by_kind.shape, 1) % SUB)
    spread[...] = jnp.where(same, by_kind, 0.0).astype(BF16)
    gain = wide_lanes(jnp.broadcast_to(gain_ref[...], (SUB, PORTS)), room)
    for p in range(PORTS):
        gains[p] = jnp.broadcast_to(gain[:, p : p + 1], (SUB, LANES))
    from_lane = iota((LANES, LANES), 0) - iota((LANES, LANES), 1)
    for j in range(2 * REACH):
        shift = (from_lane == offset_of(j)).astype(BF16)
        for s in range(2):
            shifts[j // 2, s * LANES : (s + 1) * LANES, j % 2 * LANES : (j % 2 + 1) * LANES] = shift
    zero = jnp.zeros((SUB, LANES), F32)
    for x in range(REACH):
        for c in range(COLS):
            along_x[x, c] = zero
            along_x[REACH + size_x + x, c] = zero

    def prepare(x, carry):
        for c in range(COLS):
            v = block_ref[c, x]
            along_x[REACH + x, c] = v
            along_y[x, c, 0:SUB] = v
            along_y[x, c, SUB : 2 * SUB] = v
        high, low = split(along_x[REACH + x].reshape(COLS * SUB, LANES))
        at = pl.ds(pl.multiple_of(x * COLS * SUB, COLS * SUB), COLS * SUB)
        own[at, :LANES] = high
        own[at, LANES:] = low
        return carry

    lax.fori_loop(0, size_x, prepare, 0)
    for copy in loads:
        copy.wait()

    lines = size_x * SUB

    def shift_all(n, carry):
        for s in range(2):
            part = slice(s * COLS * lines // 2, (s + 1) * COLS * lines // 2)
            shifted[n, part] = plain_dot(own[part, :], shifts[n])
        return carry

    lax.fori_loop(0, REACH, shift_all, 0)

    def hot(x, carry):
        kind = classes_ref[x]
        one = jnp.concatenate([(kind == m).astype(F32) for m in range(MAT)], axis=0).astype(BF16)
        hots[:, pl.ds(pl.multiple_of(x * LANES, LANES), LANES)] = jnp.concatenate([one, one, one], axis=0)
        return carry

    lax.fori_loop(0, size_x, hot, 0)

    def coefficients(i, carry):
        for s in range(2):
            at = pl.ds(pl.multiple_of((2 * i + s) * 2 * LANES, 2 * LANES), 2 * LANES)
            coefs[:, at] = plain_dot(spread[...], hots[:, at])
        return carry

    lax.fori_loop(0, size_x // 4, coefficients, 0)

    def plane(x, carry):
        port = ports_ref[x]
        here = pl.ds(pl.multiple_of(x * LANES, LANES), LANES)
        coef_at = lambda t: coefs[t * SUB : (t + 1) * SUB, here]
        diag = coef_at(6 * REACH)
        extra = zero
        for p in range(PORTS):
            extra = jnp.where(port == p + 1, gains[p], extra)
        diag = diag + extra
        acc = [diag * along_x[REACH + x, c] for c in range(COLS)]
        for j in range(2 * REACH):
            coef = coef_at(j)
            for c in range(COLS):
                acc[c] = acc[c] - coef * along_x[REACH + x + offset_of(j), c]
        for j in range(REACH):
            coef_x_ref[x, j] = jnp.where(x < size_x // 2, coef_at(j), coef_at(REACH + j))
        for k in range(1, REACH + 1):
            up = coef_at(2 * REACH + index_of(k))
            down = coef_at(2 * REACH + index_of(k - SUB))
            inside = row < SUB - k
            coef = jnp.where(inside, up, down)
            coef_y_ref[x, k - 1] = jnp.where(inside, down, up)
            for c in range(COLS):
                acc[c] = acc[c] - coef * along_y[x, c, k : k + SUB]
        for j in range(2 * REACH):
            coef = coef_at(4 * REACH + j)
            for c in range(COLS):
                line = pl.ds(pl.multiple_of((x * COLS + c) * SUB, SUB), SUB)
                acc[c] = acc[c] - coef * shifted[j // 2, line, j % 2 * LANES : (j % 2 + 1) * LANES]
        for c in range(COLS):
            part_ref[x, c] = acc[c]
        return carry

    lax.fori_loop(0, size_x, plane, 0)

    for copy in basis_loads:
        copy.wait()

    def store(x, carry):
        for y in range(SUB):
            high, low = split(whole[x * SUB + y])
            at = pl.ds(pl.multiple_of((x * SUB + y) * LANES, LANES), LANES)
            both_ref[:, at] = jnp.concatenate([high, low], axis=0)
        return carry

    lax.fori_loop(0, size_x, store, 0)
    halves = [both_ref[:, : lines * LANES // 2], both_ref[:, lines * LANES // 2 :]]
    products = sum(rows_dot(half, half) for half in halves)
    products = jnp.concatenate([products, jnp.zeros((2 * wide, LANES - 2 * wide), F32)], axis=1)
    products = products[:wide] + products[wide:]
    products = products + pltpu.roll(products, LANES - wide, 1)
    sums = zero
    for a in range(BLOCKS):
        block = jnp.where(lane < (a + 1) * COLS, products[a * COLS : (a + 1) * COLS], 0.0)
        sums = sums + (pltpu.roll(block, QQ_AT[a], 1) if QQ_AT[a] else block)
    sums_ref[...] = sums


def halo_kernel(part_ref, coef_x_ref, coef_y_ref, both_ref, sums_ref,
                xa_ref, xb_ref, ya_ref, yb_ref,
                w_ref, out_ref, around, outside, image, room):
    size_x = part_ref.shape[0]
    odd_x = odd_place(GX) == 1
    odd_y = odd_place(GY)
    for p in range(REACH):
        for c in range(COLS):
            first, second = xa_ref[c, p], xb_ref[c, p]
            outside[p, c] = jnp.where(odd_x, first, second)
            outside[REACH + p, c] = jnp.where(odd_x, second, first)
    at_a = pl.ds(pl.multiple_of((1 - odd_y) * SUB, SUB), SUB)
    at_b = pl.ds(pl.multiple_of(odd_y * SUB, SUB), SUB)
    lines = size_x * SUB
    for x in range(size_x):
        for c in range(COLS):
            around[x, c, at_a] = ya_ref[c, x]
            around[x, c, at_b] = yb_ref[c, x]
        acc = [part_ref[x, c] for c in range(COLS)]
        for k in range(1, REACH + 1):
            coef = coef_y_ref[x, k - 1]
            for c in range(COLS):
                acc[c] = acc[c] - coef * around[x, c, k : k + SUB]
        for j in range(2 * REACH):
            at = x + offset_of(j)
            if 0 <= at < size_x:
                continue
            coef = coef_x_ref[x, j % REACH]
            for c in range(COLS):
                value = outside[at + REACH if at < 0 else at - size_x + REACH, c]
                acc[c] = acc[c] - coef * value
        for c in range(COLS):
            image[c * lines + x * SUB : c * lines + (x + 1) * SUB, :] = acc[c]
        for y in range(SUB):
            high, low = split(image[pl.ds(x * SUB + y, COLS, stride=lines), :])
            at = (x * SUB + y) * LANES
            w_ref[:, at : at + LANES] = jnp.concatenate([high, low], axis=0)
    wide = BLOCKS * COLS
    halves = [slice(0, lines * LANES // 2), slice(lines * LANES // 2, lines * LANES)]
    lane = iota((SUB, LANES), 1)
    q_w = wide_lanes(sum(rows_dot(w_ref[:, at], both_ref[:, at]) for at in halves), room)
    q_w = q_w[:COLS] + q_w[COLS:]
    q_w = jnp.where(lane < wide, q_w + pltpu.roll(q_w, LANES - wide, 1), 0.0)
    w_w = wide_lanes(sum(rows_dot(w_ref[:, at], w_ref[:, at]) for at in halves), room)
    w_w = w_w[:COLS] + w_w[COLS:]
    w_w = jnp.where(lane < COLS, w_w + pltpu.roll(w_w, LANES - COLS, 1), 0.0)
    out_ref[...] = sums_ref[...] + pltpu.roll(q_w, QW_AT, 1) + pltpu.roll(w_w, WW_AT, 1)


def fold_kernel(*refs):
    *tiles, out_ref = refs
    total = sum(jnp.sum(tile[...], axis=0) if tile.ndim == 3 else tile[...] for tile in tiles)
    out_ref[...] = jnp.broadcast_to(total[None], out_ref.shape)


def root_inverse(value):
    guess = lax.rsqrt(value)
    return guess * (1.5 - 0.5 * value * guess * guess)


def finish_kernel(scale, taps_ref, received_ref, both_ref, w_ref,
                  next_ref, projection_ref, triangle_ref,
                  room, result, sems, projection_room, triangle_room, small_sems):
    size_x = next_ref.shape[1] // SUB
    wide = BLOCKS * COLS
    row = iota((SUB, LANES), 0)
    lane = iota((SUB, LANES), 1)
    sums = jnp.sum(received_ref[...], axis=0) * scale
    taps = wide_lanes(taps_ref[...], room)
    totals = jnp.broadcast_to(jnp.sum(taps, axis=1, keepdims=True), (MAT, LANES))
    shift = 1.0 + shift_of(totals)
    part_t = jnp.where(lane < wide, pltpu.roll(sums, LANES - QW_AT, 1), 0.0)
    w_w = jnp.where(lane < COLS, pltpu.roll(sums, LANES - WW_AT, 1), 0.0)
    blocks = []
    for a in range(BLOCKS):
        block = pltpu.roll(sums, LANES - QQ_AT[a], 1) if QQ_AT[a] else sums
        block = jnp.where(lane < (a + 1) * COLS, block, 0.0)
        last = block
        blocks.append(jnp.where(lane >= a * COLS, 0.5 * block, block))
    unit = jnp.where(lane == row + (wide - COLS), 1.0, 0.0)
    p_t = part_t + shift * last
    back_t = shift * (unit - last) - part_t
    lower = jnp.concatenate(blocks + [jnp.zeros((LANES - wide, LANES), F32)], axis=0)
    rest = jnp.zeros((LANES - SUB, LANES), F32)
    inner = part_t + plain_dot(back_t, lower, HIGHEST)
    gram = (
        w_w
        + rows_dot(inner, jnp.concatenate([back_t, rest], axis=0), HIGHEST)
        + rows_dot(back_t, jnp.concatenate([inner, rest], axis=0), HIGHEST)
    )
    apply = jnp.where(lane == row + wide, 1.0, back_t)
    every = lambda value: jnp.broadcast_to(value, (SUB, LANES))
    for k in range(0, COLS, 2):
        first, second = every(gram[:, k : k + 1]), every(gram[:, k + 1 : k + 2])
        inverse = root_inverse(every(gram[k : k + 1, k : k + 1]))
        beside = every(gram[k : k + 1, k + 1 : k + 2]) * inverse
        inverse_next = root_inverse(every(gram[k + 1 : k + 2, k + 1 : k + 2]) - beside * beside)
        first = first * inverse
        second = (second - beside * first) * inverse_next
        first = jnp.where(row > k + 1, first, 0.0)
        second = jnp.where(row > k + 1, second, 0.0)

        def step(value):
            top = every(value[k : k + 1, :]) * inverse
            low = (every(value[k + 1 : k + 2, :]) - beside * top) * inverse_next
            value = value - first * top - second * low
            return jnp.where(row == k, top, jnp.where(row == k + 1, low, value))

        gram, apply = step(gram), step(apply)
    triangle_room[...] = jnp.where(lane >= row, gram, 0.0)[:, :COLS]
    projection_room[...] = p_t[:, :wide]
    copies = [
        pltpu.make_async_copy(triangle_room, triangle_ref, small_sems.at[0]),
        pltpu.make_async_copy(projection_room, projection_ref, small_sems.at[1]),
    ]
    for copy in copies:
        copy.start()
    high, low = split(apply)
    pieces = jnp.concatenate([high.astype(F32), low.astype(F32)], axis=0)
    lane = iota(pieces.shape, 1)
    on_both = jnp.where(lane < wide, pieces, pltpu.roll(pieces, wide, 1))[:, : 2 * wide].astype(BF16)
    pieces = pltpu.roll(pieces, LANES - wide, 1)
    on_w = jnp.where(lane < COLS, pieces, pltpu.roll(pieces, COLS, 1))[:, : 2 * COLS].astype(BF16)
    group = size_x // 8
    for x in range(size_x):
        at = slice(x * SUB * LANES, (x + 1) * SUB * LANES)
        block = plain_dot(on_both, both_ref[:, at]) + plain_dot(on_w, w_ref[:, at])
        block = block[:COLS] + block[COLS:]
        for y in range(SUB):
            result[x * SUB + y] = block[:, y * LANES : (y + 1) * LANES]
        if x % group == group - 1:
            for c in range(COLS):
                copies.append(pltpu.make_async_copy(
                    result.at[pl.ds((x + 1 - group) * SUB, group * SUB), c],
                    next_ref.at[c, pl.ds((x + 1 - group) * SUB, group * SUB)],
                    sems.at[x // group, c],
                ))
                copies[-1].start()
    for copy in copies:
        copy.wait()


def swaps(devices):
    first = [(i, i ^ 1) for i in range(devices)]
    second = [pair for i in range(1, devices - 1, 2) for pair in ((i, i + 1), (i + 1, i))]
    return first, second


def per_device(basis, classes, ports, taps, port_gain):
    size_x, size_y, size_z = classes.shape
    x_first, x_second = swaps(lax.axis_size(GX))
    y_first, y_second = swaps(lax.axis_size(GY))
    shape = jax.ShapeDtypeStruct
    wide, cells, lines = BLOCKS * COLS, size_x * size_y * size_z, size_x * SUB
    tile = shape((SUB, LANES), F32)
    edge = shape((COLS, REACH, SUB, LANES), F32)
    block, xa, xb = pl.pallas_call(
        edges_kernel,
        out_shape=(shape((COLS, size_x, SUB, LANES), F32), edge, edge),
        in_specs=[HBM],
        out_specs=(VMEM,) * 3,
        scratch_shapes=[pltpu.SemaphoreType.DMA((3,))],
        compiler_params=limit(4),
        name="edges",
    )(in_hbm(basis))
    yb = lax.ppermute(block, GY, y_second)
    xb = lax.ppermute(xb, GX, x_second)
    xa = lax.ppermute(xa, GX, x_first)
    ya = lax.ppermute(block, GY, y_first)
    part, coef_x, coef_y, both, sums = pl.pallas_call(
        local_kernel,
        out_shape=(
            shape((size_x, COLS, SUB, LANES), F32),
            shape((size_x, REACH, SUB, LANES), F32),
            shape((size_x, REACH, SUB, LANES), F32),
            shape((2 * wide, cells), BF16),
            tile,
        ),
        in_specs=[VMEM, VMEM, HBM, VMEM, HBM, HBM],
        out_specs=(VMEM,) * 5,
        scratch_shapes=[
            pltpu.VMEM((size_x + 2 * REACH, COLS, SUB, LANES), F32),
            pltpu.VMEM((size_x, COLS, 2 * SUB, LANES), F32),
            pltpu.VMEM((PORTS, SUB, LANES), F32),
            pltpu.VMEM((SUB, LANES), F32),
            pltpu.VMEM(((6 * REACH + 1) * SUB, 3 * MAT * SUB), BF16),
            pltpu.VMEM((3 * MAT * SUB, size_x * LANES), BF16),
            pltpu.VMEM(((6 * REACH + 1) * SUB, size_x * LANES), F32),
            pltpu.VMEM((lines, wide, LANES), F32),
            pltpu.VMEM((COLS * lines, 2 * LANES), BF16),
            pltpu.VMEM((REACH, 2 * LANES, 2 * LANES), BF16),
            pltpu.VMEM((REACH, COLS * lines, 2 * LANES), F32),
            pltpu.VMEM((size_x, SUB, LANES), jnp.int32),
            pltpu.VMEM((size_x, SUB, LANES), jnp.int32),
            pltpu.SemaphoreType.DMA((2 + wide,)),
        ],
        compiler_params=limit(26),
        cost_estimate=pl.CostEstimate(flops=10**9, bytes_accessed=8 * 2**20, transcendentals=0),
        name="local",
    )(taps, port_gain[None], in_hbm(basis.reshape(wide, lines, LANES)), block, in_hbm(classes), in_hbm(ports))
    w, sums = pl.pallas_call(
        halo_kernel,
        out_shape=(shape((2 * COLS, cells), BF16), tile),
        in_specs=[VMEM] * 9,
        out_specs=(VMEM,) * 2,
        scratch_shapes=[
            pltpu.VMEM((size_x, COLS, 2 * SUB, LANES), F32),
            pltpu.VMEM((2 * REACH, COLS, SUB, LANES), F32),
            pltpu.VMEM((COLS * lines, LANES), F32),
            pltpu.VMEM((2 * COLS, LANES), F32),
        ],
        compiler_params=limit(8),
        name="halo",
    )(part, coef_x, coef_y, both, sums, xa, xb, ya, yb)

    def fold(copies, *tiles):
        return pl.pallas_call(
            fold_kernel,
            out_shape=shape((copies, SUB, LANES), F32),
            in_specs=[VMEM] * len(tiles),
            out_specs=VMEM,
            compiler_params=limit(2),
            name="fold",
        )(*tiles)

    beside = lax.ppermute(sums, "gy_1", [(0, 1), (1, 0)])
    along_gx = lax.all_to_all(fold(lax.axis_size(GX), sums, beside), GX, 0, 0)
    received = lax.all_to_all(fold(lax.axis_size("gy_0"), along_gx), "gy_0", 0, 0)
    total = cells * lax.axis_size(GX) * lax.axis_size(GY)
    next_block, projection, triangle = pl.pallas_call(
        functools.partial(finish_kernel, 1.0 / total),
        out_shape=(
            shape((COLS, lines, LANES), F32),
            shape((COLS, wide), F32),
            shape((COLS, COLS), F32),
        ),
        in_specs=[VMEM] * 4,
        out_specs=(HBM, HBM, HBM),
        scratch_shapes=[
            pltpu.VMEM((MAT, LANES), F32),
            pltpu.VMEM((lines, COLS, LANES), F32),
            pltpu.SemaphoreType.DMA((8, COLS)),
            pltpu.VMEM((COLS, wide), F32),
            pltpu.VMEM((COLS, COLS), F32),
            pltpu.SemaphoreType.DMA((2,)),
        ],
        compiler_params=limit(8),
        name="finish",
    )(taps, received, both, w)
    return next_block.reshape(COLS, size_x, size_y, size_z), projection.T, triangle


def solution(mesh):
    split_mesh = Mesh(mesh.devices.reshape(4, 8, 16, 2), AXES)
    in_specs = (P(None, GX, GY, None), P(GX, GY, None), P(GX, GY, None), P(), P())
    out_specs = (P(None, GX, GY, None), P(), P())
    return jax.shard_map(
        per_device, mesh=split_mesh, in_specs=in_specs, out_specs=out_specs, check_vma=False
    )
```

```python
import functools

import jax
import jax.numpy as jnp
from jax import lax
from jax.experimental import pallas as pl
from jax.experimental.pallas import tpu as pltpu
from jax.sharding import Mesh
from jax.sharding import PartitionSpec as P

COLS = 8
BLOCKS = 4
REACH = 7
MAT = 8
PORTS = 8
AXES = ("gx_0", "gx_1", "gy_0", "gy_1")
GX = ("gx_0", "gx_1")
GY = ("gy_0", "gy_1")
SUB = 8
LANES = 128
HIGHEST = lax.Precision.HIGHEST
F32 = jnp.float32
BF16 = jnp.bfloat16
VMEM = pl.BlockSpec(memory_space=pltpu.VMEM)
HBM = pl.BlockSpec(memory_space=pltpu.MemorySpace.HBM)

QQ_AT = (0, 8, 24, 48)
QW_AT = 80
WW_AT = 112


def in_hbm(value):
    return pltpu.with_memory_space_constraint(value, pltpu.MemorySpace.HBM)


def limit(mebibytes):
    return pltpu.CompilerParams(vmem_limit_bytes=mebibytes * 2**20)


def offset_of(j):
    return j - REACH if j < REACH else j - REACH + 1


def index_of(k):
    return k + REACH if k < 0 else k + REACH - 1


def iota(shape, dim):
    return lax.broadcasted_iota(jnp.int32, shape, dim)


def split(value):
    high = value.astype(BF16)
    return high, (value - high.astype(F32)).astype(BF16)


def rows_dot(a, b, precision=None):
    return lax.dot_general(
        a, b, (((1,), (1,)), ((), ())), precision=precision, preferred_element_type=F32
    )


def plain_dot(a, b, precision=None):
    return lax.dot_general(
        a, b, (((1,), (0,)), ((), ())), precision=precision, preferred_element_type=F32
    )


def shift_of(totals):
    return jnp.mean(totals, axis=0, keepdims=True)


def wide_lanes(value, room):
    room[...] = jnp.zeros(room.shape, F32)
    room[:, : value.shape[1]] = value
    return room[...]


def odd_place(axes):
    place = 0
    for axis in axes:
        place = place * lax.axis_size(axis) + lax.axis_index(axis)
    return lax.rem(place, 2)


def edges_kernel(basis_ref, block_ref, xa_ref, xb_ref, sems):
    odd = odd_place(GX)
    block = basis_ref.at[(BLOCKS - 1) * COLS : BLOCKS * COLS]
    far = basis_ref.shape[1] - REACH
    jobs = (
        (block, block_ref),
        (block.at[:, pl.ds((1 - odd) * far, REACH)], xa_ref),
        (block.at[:, pl.ds(odd * far, REACH)], xb_ref),
    )
    copies = [pltpu.make_async_copy(*job, sems.at[i]) for i, job in enumerate(jobs)]
    for copy in copies:
        copy.start()
    for copy in copies:
        copy.wait()


def local_kernel(taps_ref, gain_ref, basis_ref, block_ref, classes_hbm, ports_hbm,
                 part_ref, coef_x_ref, coef_y_ref, both_ref, sums_ref,
                 along_x, along_y, gains, room, spread, coefs, whole,
                 classes_ref, ports_ref, sems):
    size_x = classes_ref.shape[0]
    wide = BLOCKS * COLS
    jobs = ((classes_hbm, classes_ref), (ports_hbm, ports_ref))
    loads = [pltpu.make_async_copy(*job, sems.at[i]) for i, job in enumerate(jobs)]
    basis_loads = [pltpu.make_async_copy(basis_ref.at[c], whole.at[:, c], sems.at[2 + c]) for c in range(wide)]
    for copy in (*loads, *basis_loads):
        copy.start()
    row = iota((SUB, LANES), 0)
    lane = iota((SUB, LANES), 1)
    taps = wide_lanes(taps_ref[...], room)
    totals = jnp.broadcast_to(jnp.sum(taps, axis=1, keepdims=True), (MAT, LANES))
    taps = jnp.where(lane == 6 * REACH, totals - shift_of(totals), taps)
    high, _ = split(taps)
    middle, low = split((taps - high.astype(F32)))
    each = jnp.concatenate([high.astype(F32), middle.astype(F32), low.astype(F32)], axis=0)
    each = jnp.broadcast_to(each[:, None, :], (3 * MAT, SUB, LANES)).reshape(3 * MAT * SUB, LANES)
    count = 6 * REACH + 1
    chosen = (iota((count * SUB, LANES), 0) // SUB == iota((count * SUB, LANES), 1)).astype(BF16)
    by_kind = rows_dot(chosen, each.astype(BF16))
    same = (iota(by_kind.shape, 0) % SUB) == (iota(by_kind.shape, 1) % SUB)
    spread[...] = jnp.where(same, by_kind, 0.0).astype(BF16)
    gain = wide_lanes(jnp.broadcast_to(gain_ref[...], (SUB, PORTS)), room)
    for p in range(PORTS):
        gains[p] = jnp.broadcast_to(gain[:, p : p + 1], (SUB, LANES))
    zero = jnp.zeros((SUB, LANES), F32)
    for x in range(REACH):
        for c in range(COLS):
            along_x[x, c] = zero
            along_x[REACH + size_x + x, c] = zero

    def prepare(x, carry):
        for c in range(COLS):
            v = block_ref[c, x]
            along_x[REACH + x, c] = v
            along_y[x, c, 0:SUB] = v
            along_y[x, c, SUB : 2 * SUB] = v
        return carry

    lax.fori_loop(0, size_x, prepare, 0)
    for copy in loads:
        copy.wait()

    lines = size_x * SUB

    def coefficients(x):
        kind = classes_ref[x]
        one = jnp.concatenate([(kind == m).astype(F32) for m in range(MAT)], axis=0).astype(BF16)
        return plain_dot(spread[...], jnp.concatenate([one, one, one], axis=0))

    coefs[...] = coefficients(0)

    def plane(x, carry):
        port = ports_ref[x]
        own = [along_x[REACH + x, c] for c in range(COLS)]
        later = coefficients(jnp.minimum(x + 1, size_x - 1))
        coef_at = lambda t: coefs[t * SUB : (t + 1) * SUB, :]
        diag = coef_at(6 * REACH)
        extra = zero
        for p in range(PORTS):
            extra = jnp.where(port == p + 1, gains[p], extra)
        diag = diag + extra
        acc = [diag * v for v in own]
        for j in range(2 * REACH):
            coef = coef_at(j)
            for c in range(COLS):
                acc[c] = acc[c] - coef * along_x[REACH + x + offset_of(j), c]
        for j in range(REACH):
            coef_x_ref[x, j] = jnp.where(x < size_x // 2, coef_at(j), coef_at(REACH + j))
        for k in range(1, REACH + 1):
            up = coef_at(2 * REACH + index_of(k))
            down = coef_at(2 * REACH + index_of(k - SUB))
            inside = row < SUB - k
            coef = jnp.where(inside, up, down)
            coef_y_ref[x, k - 1] = jnp.where(inside, down, up)
            for c in range(COLS):
                acc[c] = acc[c] - coef * along_y[x, c, k : k + SUB]
        for j in range(2 * REACH):
            k = offset_of(j)
            coef = jnp.where((lane + k >= 0) & (lane + k < LANES), coef_at(4 * REACH + j), 0.0)
            for c in range(COLS):
                acc[c] = acc[c] - coef * pltpu.roll(own[c], (-k) % LANES, 1)
        for c in range(COLS):
            part_ref[x, c] = acc[c]
        coefs[...] = later
        return carry

    lax.fori_loop(0, size_x, plane, 0)

    for copy in basis_loads:
        copy.wait()

    def store(x, carry):
        for y in range(SUB):
            high, low = split(whole[x * SUB + y])
            at = pl.ds(pl.multiple_of((x * SUB + y) * LANES, LANES), LANES)
            both_ref[:, at] = jnp.concatenate([high, low], axis=0)
        return carry

    lax.fori_loop(0, size_x, store, 0)
    halves = [both_ref[:, : lines * LANES // 2], both_ref[:, lines * LANES // 2 :]]
    products = sum(rows_dot(half, half) for half in halves)
    products = jnp.concatenate([products, jnp.zeros((2 * wide, LANES - 2 * wide), F32)], axis=1)
    products = products[:wide] + products[wide:]
    products = products + pltpu.roll(products, LANES - wide, 1)
    sums = zero
    for a in range(BLOCKS):
        block = jnp.where(lane < (a + 1) * COLS, products[a * COLS : (a + 1) * COLS], 0.0)
        sums = sums + (pltpu.roll(block, QQ_AT[a], 1) if QQ_AT[a] else block)
    sums_ref[...] = sums


def halo_kernel(part_ref, coef_x_ref, coef_y_ref, both_ref, sums_ref,
                xa_ref, xb_ref, ya_ref, yb_ref,
                w_ref, out_ref, around, outside, image, room):
    size_x = part_ref.shape[0]
    odd_x = odd_place(GX) == 1
    odd_y = odd_place(GY)
    for p in range(REACH):
        for c in range(COLS):
            first, second = xa_ref[c, p], xb_ref[c, p]
            outside[p, c] = jnp.where(odd_x, first, second)
            outside[REACH + p, c] = jnp.where(odd_x, second, first)
    at_a = pl.ds(pl.multiple_of((1 - odd_y) * SUB, SUB), SUB)
    at_b = pl.ds(pl.multiple_of(odd_y * SUB, SUB), SUB)
    lines = size_x * SUB
    for x in range(size_x):
        for c in range(COLS):
            around[x, c, at_a] = ya_ref[c, x]
            around[x, c, at_b] = yb_ref[c, x]
        acc = [part_ref[x, c] for c in range(COLS)]
        for k in range(1, REACH + 1):
            coef = coef_y_ref[x, k - 1]
            for c in range(COLS):
                acc[c] = acc[c] - coef * around[x, c, k : k + SUB]
        for j in range(2 * REACH):
            at = x + offset_of(j)
            if 0 <= at < size_x:
                continue
            coef = coef_x_ref[x, j % REACH]
            for c in range(COLS):
                value = outside[at + REACH if at < 0 else at - size_x + REACH, c]
                acc[c] = acc[c] - coef * value
        for c in range(COLS):
            image[c * lines + x * SUB : c * lines + (x + 1) * SUB, :] = acc[c]
        for y in range(SUB):
            high, low = split(image[pl.ds(x * SUB + y, COLS, stride=lines), :])
            at = (x * SUB + y) * LANES
            w_ref[:, at : at + LANES] = jnp.concatenate([high, low], axis=0)
    wide = BLOCKS * COLS
    halves = [slice(0, lines * LANES // 2), slice(lines * LANES // 2, lines * LANES)]
    lane = iota((SUB, LANES), 1)
    q_w = wide_lanes(sum(rows_dot(w_ref[:, at], both_ref[:, at]) for at in halves), room)
    q_w = q_w[:COLS] + q_w[COLS:]
    q_w = jnp.where(lane < wide, q_w + pltpu.roll(q_w, LANES - wide, 1), 0.0)
    w_w = wide_lanes(sum(rows_dot(w_ref[:, at], w_ref[:, at]) for at in halves), room)
    w_w = w_w[:COLS] + w_w[COLS:]
    w_w = jnp.where(lane < COLS, w_w + pltpu.roll(w_w, LANES - COLS, 1), 0.0)
    out_ref[...] = sums_ref[...] + pltpu.roll(q_w, QW_AT, 1) + pltpu.roll(w_w, WW_AT, 1)


def fold_kernel(*refs):
    *tiles, out_ref = refs
    total = sum(jnp.sum(tile[...], axis=0) if tile.ndim == 3 else tile[...] for tile in tiles)
    out_ref[...] = jnp.broadcast_to(total[None], out_ref.shape)


def root_inverse(value):
    guess = lax.rsqrt(value)
    return guess * (1.5 - 0.5 * value * guess * guess)


def finish_kernel(scale, taps_ref, received_ref, both_ref, w_ref,
                  next_ref, projection_ref, triangle_ref,
                  room, result, sems, projection_room, triangle_room, small_sems):
    size_x = next_ref.shape[1] // SUB
    wide = BLOCKS * COLS
    row = iota((SUB, LANES), 0)
    lane = iota((SUB, LANES), 1)
    sums = jnp.sum(received_ref[...], axis=0) * scale
    taps = wide_lanes(taps_ref[...], room)
    totals = jnp.broadcast_to(jnp.sum(taps, axis=1, keepdims=True), (MAT, LANES))
    shift = 1.0 + shift_of(totals)
    part_t = jnp.where(lane < wide, pltpu.roll(sums, LANES - QW_AT, 1), 0.0)
    w_w = jnp.where(lane < COLS, pltpu.roll(sums, LANES - WW_AT, 1), 0.0)
    blocks = []
    for a in range(BLOCKS):
        block = pltpu.roll(sums, LANES - QQ_AT[a], 1) if QQ_AT[a] else sums
        block = jnp.where(lane < (a + 1) * COLS, block, 0.0)
        last = block
        blocks.append(jnp.where(lane >= a * COLS, 0.5 * block, block))
    unit = jnp.where(lane == row + (wide - COLS), 1.0, 0.0)
    p_t = part_t + shift * last
    back_t = shift * (unit - last) - part_t
    lower = jnp.concatenate(blocks + [jnp.zeros((LANES - wide, LANES), F32)], axis=0)
    rest = jnp.zeros((LANES - SUB, LANES), F32)
    inner = part_t + plain_dot(back_t, lower, HIGHEST)
    gram = (
        w_w
        + rows_dot(inner, jnp.concatenate([back_t, rest], axis=0), HIGHEST)
        + rows_dot(back_t, jnp.concatenate([inner, rest], axis=0), HIGHEST)
    )
    apply = jnp.where(lane == row + wide, 1.0, back_t)
    every = lambda value: jnp.broadcast_to(value, (SUB, LANES))
    for k in range(0, COLS, 2):
        first, second = every(gram[:, k : k + 1]), every(gram[:, k + 1 : k + 2])
        inverse = root_inverse(every(gram[k : k + 1, k : k + 1]))
        beside = every(gram[k : k + 1, k + 1 : k + 2]) * inverse
        inverse_next = root_inverse(every(gram[k + 1 : k + 2, k + 1 : k + 2]) - beside * beside)
        first = first * inverse
        second = (second - beside * first) * inverse_next
        first = jnp.where(row > k + 1, first, 0.0)
        second = jnp.where(row > k + 1, second, 0.0)

        def step(value):
            top = every(value[k : k + 1, :]) * inverse
            low = (every(value[k + 1 : k + 2, :]) - beside * top) * inverse_next
            value = value - first * top - second * low
            return jnp.where(row == k, top, jnp.where(row == k + 1, low, value))

        gram, apply = step(gram), step(apply)
    triangle_room[...] = jnp.where(lane >= row, gram, 0.0)[:, :COLS]
    projection_room[...] = p_t[:, :wide]
    copies = [
        pltpu.make_async_copy(triangle_room, triangle_ref, small_sems.at[0]),
        pltpu.make_async_copy(projection_room, projection_ref, small_sems.at[1]),
    ]
    for copy in copies:
        copy.start()
    high, low = split(apply)
    pieces = jnp.concatenate([high.astype(F32), low.astype(F32)], axis=0)
    lane = iota(pieces.shape, 1)
    on_both = jnp.where(lane < wide, pieces, pltpu.roll(pieces, wide, 1))[:, : 2 * wide].astype(BF16)
    pieces = pltpu.roll(pieces, LANES - wide, 1)
    on_w = jnp.where(lane < COLS, pieces, pltpu.roll(pieces, COLS, 1))[:, : 2 * COLS].astype(BF16)
    group = size_x // 8
    for x in range(size_x):
        at = slice(x * SUB * LANES, (x + 1) * SUB * LANES)
        block = plain_dot(on_both, both_ref[:, at]) + plain_dot(on_w, w_ref[:, at])
        block = block[:COLS] + block[COLS:]
        for y in range(SUB):
            result[x * SUB + y] = block[:, y * LANES : (y + 1) * LANES]
        if x % group == group - 1:
            for c in range(COLS):
                copies.append(pltpu.make_async_copy(
                    result.at[pl.ds((x + 1 - group) * SUB, group * SUB), c],
                    next_ref.at[c, pl.ds((x + 1 - group) * SUB, group * SUB)],
                    sems.at[x // group, c],
                ))
                copies[-1].start()
    for copy in copies:
        copy.wait()


def swaps(devices):
    first = [(i, i ^ 1) for i in range(devices)]
    second = [pair for i in range(1, devices - 1, 2) for pair in ((i, i + 1), (i + 1, i))]
    return first, second


def per_device(basis, classes, ports, taps, port_gain):
    size_x, size_y, size_z = classes.shape
    x_first, x_second = swaps(lax.axis_size(GX))
    y_first, y_second = swaps(lax.axis_size(GY))
    shape = jax.ShapeDtypeStruct
    wide, cells, lines = BLOCKS * COLS, size_x * size_y * size_z, size_x * SUB
    tile = shape((SUB, LANES), F32)
    edge = shape((COLS, REACH, SUB, LANES), F32)
    block, xa, xb = pl.pallas_call(
        edges_kernel,
        out_shape=(shape((COLS, size_x, SUB, LANES), F32), edge, edge),
        in_specs=[HBM],
        out_specs=(VMEM,) * 3,
        scratch_shapes=[pltpu.SemaphoreType.DMA((3,))],
        compiler_params=limit(4),
        name="edges",
    )(in_hbm(basis))
    yb = lax.ppermute(block, GY, y_second)
    xb = lax.ppermute(xb, GX, x_second)
    xa = lax.ppermute(xa, GX, x_first)
    ya = lax.ppermute(block, GY, y_first)
    part, coef_x, coef_y, both, sums = pl.pallas_call(
        local_kernel,
        out_shape=(
            shape((size_x, COLS, SUB, LANES), F32),
            shape((size_x, REACH, SUB, LANES), F32),
            shape((size_x, REACH, SUB, LANES), F32),
            shape((2 * wide, cells), BF16),
            tile,
        ),
        in_specs=[VMEM, VMEM, HBM, VMEM, HBM, HBM],
        out_specs=(VMEM,) * 5,
        scratch_shapes=[
            pltpu.VMEM((size_x + 2 * REACH, COLS, SUB, LANES), F32),
            pltpu.VMEM((size_x, COLS, 2 * SUB, LANES), F32),
            pltpu.VMEM((PORTS, SUB, LANES), F32),
            pltpu.VMEM((SUB, LANES), F32),
            pltpu.VMEM(((6 * REACH + 1) * SUB, 3 * MAT * SUB), BF16),
            pltpu.VMEM(((6 * REACH + 1) * SUB, LANES), F32),
            pltpu.VMEM((lines, wide, LANES), F32),
            pltpu.VMEM((size_x, SUB, LANES), jnp.int32),
            pltpu.VMEM((size_x, SUB, LANES), jnp.int32),
            pltpu.SemaphoreType.DMA((2 + wide,)),
        ],
        compiler_params=limit(16),
        cost_estimate=pl.CostEstimate(flops=10**9, bytes_accessed=8 * 2**20, transcendentals=0),
        name="local",
    )(taps, port_gain[None], in_hbm(basis.reshape(wide, lines, LANES)), block, in_hbm(classes), in_hbm(ports))
    w, sums = pl.pallas_call(
        halo_kernel,
        out_shape=(shape((2 * COLS, cells), BF16), tile),
        in_specs=[VMEM] * 9,
        out_specs=(VMEM,) * 2,
        scratch_shapes=[
            pltpu.VMEM((size_x, COLS, 2 * SUB, LANES), F32),
            pltpu.VMEM((2 * REACH, COLS, SUB, LANES), F32),
            pltpu.VMEM((COLS * lines, LANES), F32),
            pltpu.VMEM((2 * COLS, LANES), F32),
        ],
        compiler_params=limit(8),
        name="halo",
    )(part, coef_x, coef_y, both, sums, xa, xb, ya, yb)

    def fold(copies, *tiles):
        return pl.pallas_call(
            fold_kernel,
            out_shape=shape((copies, SUB, LANES), F32),
            in_specs=[VMEM] * len(tiles),
            out_specs=VMEM,
            compiler_params=limit(2),
            name="fold",
        )(*tiles)

    beside = lax.ppermute(sums, "gy_1", [(0, 1), (1, 0)])
    along_gx = lax.all_to_all(fold(lax.axis_size(GX), sums, beside), GX, 0, 0)
    received = lax.all_to_all(fold(lax.axis_size("gy_0"), along_gx), "gy_0", 0, 0)
    total = cells * lax.axis_size(GX) * lax.axis_size(GY)
    next_block, projection, triangle = pl.pallas_call(
        functools.partial(finish_kernel, 1.0 / total),
        out_shape=(
            shape((COLS, lines, LANES), F32),
            shape((COLS, wide), F32),
            shape((COLS, COLS), F32),
        ),
        in_specs=[VMEM] * 4,
        out_specs=(HBM, HBM, HBM),
        scratch_shapes=[
            pltpu.VMEM((MAT, LANES), F32),
            pltpu.VMEM((lines, COLS, LANES), F32),
            pltpu.SemaphoreType.DMA((8, COLS)),
            pltpu.VMEM((COLS, wide), F32),
            pltpu.VMEM((COLS, COLS), F32),
            pltpu.SemaphoreType.DMA((2,)),
        ],
        compiler_params=limit(8),
        name="finish",
    )(taps, received, both, w)
    return next_block.reshape(COLS, size_x, size_y, size_z), projection.T, triangle


def solution(mesh):
    split_mesh = Mesh(mesh.devices.reshape(4, 8, 16, 2), AXES)
    in_specs = (P(None, GX, GY, None), P(GX, GY, None), P(GX, GY, None), P(), P())
    out_specs = (P(None, GX, GY, None), P(), P())
    return jax.shard_map(
        per_device, mesh=split_mesh, in_specs=in_specs, out_specs=out_specs, check_vma=False
    )
```

```python
import functools

import jax
import jax.numpy as jnp
from jax import lax
from jax.experimental import pallas as pl
from jax.experimental.pallas import tpu as pltpu
from jax.sharding import Mesh
from jax.sharding import PartitionSpec as P

COLS = 8
BLOCKS = 4
REACH = 7
MAT = 8
PORTS = 8
AXES = ("gx_0", "gx_1", "gy_0", "gy_1")
GX = ("gx_0", "gx_1")
GY = ("gy_0", "gy_1")
SUB = 8
LANES = 128
HIGHEST = lax.Precision.HIGHEST
F32 = jnp.float32
BF16 = jnp.bfloat16
VMEM = pl.BlockSpec(memory_space=pltpu.VMEM)
HBM = pl.BlockSpec(memory_space=pltpu.MemorySpace.HBM)

QQ_AT = (0, 8, 24, 48)
QW_AT = 80
WW_AT = 112


def in_hbm(value):
    return pltpu.with_memory_space_constraint(value, pltpu.MemorySpace.HBM)


def limit(mebibytes):
    return pltpu.CompilerParams(vmem_limit_bytes=mebibytes * 2**20)


def offset_of(j):
    return j - REACH if j < REACH else j - REACH + 1


def index_of(k):
    return k + REACH if k < 0 else k + REACH - 1


def iota(shape, dim):
    return lax.broadcasted_iota(jnp.int32, shape, dim)


def split(value):
    high = value.astype(BF16)
    return high, (value - high.astype(F32)).astype(BF16)


def rows_dot(a, b, precision=None):
    return lax.dot_general(
        a, b, (((1,), (1,)), ((), ())), precision=precision, preferred_element_type=F32
    )


def plain_dot(a, b, precision=None):
    return lax.dot_general(
        a, b, (((1,), (0,)), ((), ())), precision=precision, preferred_element_type=F32
    )


def shift_of(totals):
    return jnp.mean(totals, axis=0, keepdims=True)


def wide_lanes(value, room):
    room[...] = jnp.zeros(room.shape, F32)
    room[:, : value.shape[1]] = value
    return room[...]


def odd_place(axes):
    place = 0
    for axis in axes:
        place = place * lax.axis_size(axis) + lax.axis_index(axis)
    return lax.rem(place, 2)


def edges_kernel(basis_ref, block_ref, xa_ref, xb_ref, sems):
    odd = odd_place(GX)
    block = basis_ref.at[(BLOCKS - 1) * COLS : BLOCKS * COLS]
    far = basis_ref.shape[1] - REACH
    jobs = (
        (block, block_ref),
        (block.at[:, pl.ds((1 - odd) * far, REACH)], xa_ref),
        (block.at[:, pl.ds(odd * far, REACH)], xb_ref),
    )
    copies = [pltpu.make_async_copy(*job, sems.at[i]) for i, job in enumerate(jobs)]
    for copy in copies:
        copy.start()
    for copy in copies:
        copy.wait()


def local_kernel(taps_ref, gain_ref, basis_ref, block_ref, classes_hbm, ports_hbm,
                 part_ref, coef_x_ref, coef_y_ref, both_ref, sums_ref,
                 along_x, along_y, gains, room, spread, coefs, whole,
                 classes_ref, ports_ref, sems):
    size_x = classes_ref.shape[0]
    wide = BLOCKS * COLS
    jobs = ((classes_hbm, classes_ref), (ports_hbm, ports_ref))
    loads = [pltpu.make_async_copy(*job, sems.at[i]) for i, job in enumerate(jobs)]
    basis_loads = [pltpu.make_async_copy(basis_ref.at[c], whole.at[:, c], sems.at[2 + c]) for c in range(wide)]
    for copy in (*loads, *basis_loads):
        copy.start()
    row = iota((SUB, LANES), 0)
    lane = iota((SUB, LANES), 1)
    taps = wide_lanes(taps_ref[...], room)
    totals = jnp.broadcast_to(jnp.sum(taps, axis=1, keepdims=True), (MAT, LANES))
    taps = jnp.where(lane == 6 * REACH, totals - shift_of(totals), taps)
    high, _ = split(taps)
    middle, low = split((taps - high.astype(F32)))
    each = jnp.concatenate([high.astype(F32), middle.astype(F32), low.astype(F32)], axis=0)
    each = jnp.broadcast_to(each[:, None, :], (3 * MAT, SUB, LANES)).reshape(3 * MAT * SUB, LANES)
    count = 6 * REACH + 1
    chosen = (iota((count * SUB, LANES), 0) // SUB == iota((count * SUB, LANES), 1)).astype(BF16)
    by_kind = rows_dot(chosen, each.astype(BF16))
    same = (iota(by_kind.shape, 0) % SUB) == (iota(by_kind.shape, 1) % SUB)
    spread[...] = jnp.where(same, by_kind, 0.0).astype(BF16)
    gain = wide_lanes(jnp.broadcast_to(gain_ref[...], (SUB, PORTS)), room)
    for p in range(PORTS):
        gains[p] = jnp.broadcast_to(gain[:, p : p + 1], (SUB, LANES))
    zero = jnp.zeros((SUB, LANES), F32)
    for x in range(REACH):
        for c in range(COLS):
            along_x[x, c] = zero
            along_x[REACH + size_x + x, c] = zero

    def prepare(x, carry):
        for c in range(COLS):
            v = block_ref[c, x]
            along_x[REACH + x, c] = v
            along_y[x, c, 0:SUB] = v
            along_y[x, c, SUB : 2 * SUB] = v
        return carry

    lax.fori_loop(0, size_x, prepare, 0)
    for copy in loads:
        copy.wait()

    lines = size_x * SUB

    def coefficients(x):
        kind = classes_ref[x]
        one = jnp.concatenate([(kind == m).astype(F32) for m in range(MAT)], axis=0).astype(BF16)
        return plain_dot(spread[...], jnp.concatenate([one, one, one], axis=0))

    coefs[...] = coefficients(0)

    def plane(x, carry):
        port = ports_ref[x]
        own = [along_x[REACH + x, c] for c in range(COLS)]
        later = coefficients(jnp.minimum(x + 1, size_x - 1))
        coef_at = lambda t: coefs[t * SUB : (t + 1) * SUB, :]
        diag = coef_at(6 * REACH)
        extra = zero
        for p in range(PORTS):
            extra = jnp.where(port == p + 1, gains[p], extra)
        diag = diag + extra
        acc = [diag * v for v in own]
        for j in range(2 * REACH):
            coef = coef_at(j)
            for c in range(COLS):
                acc[c] = acc[c] - coef * along_x[REACH + x + offset_of(j), c]
        for j in range(REACH):
            coef_x_ref[x, j] = jnp.where(x < size_x // 2, coef_at(j), coef_at(REACH + j))
        for k in range(1, REACH + 1):
            up = coef_at(2 * REACH + index_of(k))
            down = coef_at(2 * REACH + index_of(k - SUB))
            inside = row < SUB - k
            coef = jnp.where(inside, up, down)
            coef_y_ref[x, k - 1] = jnp.where(inside, down, up)
            for c in range(COLS):
                acc[c] = acc[c] - coef * along_y[x, c, k : k + SUB]
        for j in range(2 * REACH):
            k = offset_of(j)
            coef = jnp.where((lane + k >= 0) & (lane + k < LANES), coef_at(4 * REACH + j), 0.0)
            for c in range(COLS):
                acc[c] = acc[c] - coef * pltpu.roll(own[c], (-k) % LANES, 1)
        for c in range(COLS):
            part_ref[x, c] = acc[c]
        coefs[...] = later
        return carry

    lax.fori_loop(0, size_x, plane, 0, unroll=2)

    for copy in basis_loads:
        copy.wait()

    def store(x, carry):
        for y in range(SUB):
            high, low = split(whole[x * SUB + y])
            at = pl.ds(pl.multiple_of((x * SUB + y) * LANES, LANES), LANES)
            both_ref[:, at] = jnp.concatenate([high, low], axis=0)
        return carry

    lax.fori_loop(0, size_x, store, 0)
    halves = [both_ref[:, : lines * LANES // 2], both_ref[:, lines * LANES // 2 :]]
    products = sum(rows_dot(half, half) for half in halves)
    products = jnp.concatenate([products, jnp.zeros((2 * wide, LANES - 2 * wide), F32)], axis=1)
    products = products[:wide] + products[wide:]
    products = products + pltpu.roll(products, LANES - wide, 1)
    sums = zero
    for a in range(BLOCKS):
        block = jnp.where(lane < (a + 1) * COLS, products[a * COLS : (a + 1) * COLS], 0.0)
        sums = sums + (pltpu.roll(block, QQ_AT[a], 1) if QQ_AT[a] else block)
    sums_ref[...] = sums


def halo_kernel(part_ref, coef_x_ref, coef_y_ref, both_ref, sums_ref,
                xa_ref, xb_ref, ya_ref, yb_ref,
                w_ref, out_ref, around, outside, room):
    size_x = part_ref.shape[0]
    odd_x = odd_place(GX) == 1
    odd_y = odd_place(GY)
    for p in range(REACH):
        for c in range(COLS):
            first, second = xa_ref[c, p], xb_ref[c, p]
            outside[p, c] = jnp.where(odd_x, first, second)
            outside[REACH + p, c] = jnp.where(odd_x, second, first)
    at_a = pl.ds(pl.multiple_of((1 - odd_y) * SUB, SUB), SUB)
    at_b = pl.ds(pl.multiple_of(odd_y * SUB, SUB), SUB)
    lines = size_x * SUB
    for x in range(size_x):
        for c in range(COLS):
            around[x, c, at_a] = ya_ref[c, x]
            around[x, c, at_b] = yb_ref[c, x]
        acc = [part_ref[x, c] for c in range(COLS)]
        for k in range(1, REACH + 1):
            coef = coef_y_ref[x, k - 1]
            for c in range(COLS):
                acc[c] = acc[c] - coef * around[x, c, k : k + SUB]
        for j in range(2 * REACH):
            at = x + offset_of(j)
            if 0 <= at < size_x:
                continue
            coef = coef_x_ref[x, j % REACH]
            for c in range(COLS):
                value = outside[at + REACH if at < 0 else at - size_x + REACH, c]
                acc[c] = acc[c] - coef * value
        by_line = jnp.swapaxes(jnp.stack(acc), 0, 1)
        for y in range(SUB):
            high, low = split(by_line[y])
            at = (x * SUB + y) * LANES
            w_ref[:, at : at + LANES] = jnp.concatenate([high, low], axis=0)
    wide = BLOCKS * COLS
    halves = [slice(0, lines * LANES // 2), slice(lines * LANES // 2, lines * LANES)]
    lane = iota((SUB, LANES), 1)
    q_w = wide_lanes(sum(rows_dot(w_ref[:, at], both_ref[:, at]) for at in halves), room)
    q_w = q_w[:COLS] + q_w[COLS:]
    q_w = jnp.where(lane < wide, q_w + pltpu.roll(q_w, LANES - wide, 1), 0.0)
    w_w = wide_lanes(sum(rows_dot(w_ref[:, at], w_ref[:, at]) for at in halves), room)
    w_w = w_w[:COLS] + w_w[COLS:]
    w_w = jnp.where(lane < COLS, w_w + pltpu.roll(w_w, LANES - COLS, 1), 0.0)
    out_ref[...] = sums_ref[...] + pltpu.roll(q_w, QW_AT, 1) + pltpu.roll(w_w, WW_AT, 1)


def fold_kernel(*refs):
    *tiles, out_ref = refs
    total = sum(jnp.sum(tile[...], axis=0) if tile.ndim == 3 else tile[...] for tile in tiles)
    out_ref[...] = jnp.broadcast_to(total[None], out_ref.shape)


def root_inverse(value):
    guess = lax.rsqrt(value)
    return guess * (1.5 - 0.5 * value * guess * guess)


def finish_kernel(scale, taps_ref, received_ref, both_ref, w_ref,
                  next_ref, projection_ref, triangle_ref,
                  room, result, sems, projection_room, triangle_room, small_sems):
    size_x = next_ref.shape[1] // SUB
    wide = BLOCKS * COLS
    row = iota((SUB, LANES), 0)
    lane = iota((SUB, LANES), 1)
    sums = jnp.sum(received_ref[...], axis=0) * scale
    taps = wide_lanes(taps_ref[...], room)
    totals = jnp.broadcast_to(jnp.sum(taps, axis=1, keepdims=True), (MAT, LANES))
    shift = 1.0 + shift_of(totals)
    part_t = jnp.where(lane < wide, pltpu.roll(sums, LANES - QW_AT, 1), 0.0)
    w_w = jnp.where(lane < COLS, pltpu.roll(sums, LANES - WW_AT, 1), 0.0)
    blocks = []
    for a in range(BLOCKS):
        block = pltpu.roll(sums, LANES - QQ_AT[a], 1) if QQ_AT[a] else sums
        block = jnp.where(lane < (a + 1) * COLS, block, 0.0)
        last = block
        blocks.append(jnp.where(lane >= a * COLS, 0.5 * block, block))
    unit = jnp.where(lane == row + (wide - COLS), 1.0, 0.0)
    p_t = part_t + shift * last
    back_t = shift * (unit - last) - part_t
    lower = jnp.concatenate(blocks + [jnp.zeros((LANES - wide, LANES), F32)], axis=0)
    rest = jnp.zeros((LANES - SUB, LANES), F32)
    inner = part_t + plain_dot(back_t, lower, HIGHEST)
    gram = (
        w_w
        + rows_dot(inner, jnp.concatenate([back_t, rest], axis=0), HIGHEST)
        + rows_dot(back_t, jnp.concatenate([inner, rest], axis=0), HIGHEST)
    )
    apply = jnp.where(lane == row + wide, 1.0, back_t)
    every = lambda value: jnp.broadcast_to(value, (SUB, LANES))
    for k in range(0, COLS, 2):
        first, second = every(gram[:, k : k + 1]), every(gram[:, k + 1 : k + 2])
        inverse = root_inverse(every(gram[k : k + 1, k : k + 1]))
        beside = every(gram[k : k + 1, k + 1 : k + 2]) * inverse
        inverse_next = root_inverse(every(gram[k + 1 : k + 2, k + 1 : k + 2]) - beside * beside)
        first = first * inverse
        second = (second - beside * first) * inverse_next
        first = jnp.where(row > k + 1, first, 0.0)
        second = jnp.where(row > k + 1, second, 0.0)

        def step(value):
            top = every(value[k : k + 1, :]) * inverse
            low = (every(value[k + 1 : k + 2, :]) - beside * top) * inverse_next
            value = value - first * top - second * low
            return jnp.where(row == k, top, jnp.where(row == k + 1, low, value))

        gram, apply = step(gram), step(apply)
    triangle_room[...] = jnp.where(lane >= row, gram, 0.0)[:, :COLS]
    projection_room[...] = p_t[:, :wide]
    copies = [
        pltpu.make_async_copy(triangle_room, triangle_ref, small_sems.at[0]),
        pltpu.make_async_copy(projection_room, projection_ref, small_sems.at[1]),
    ]
    for copy in copies:
        copy.start()
    high, low = split(apply)
    pieces = jnp.concatenate([high.astype(F32), low.astype(F32)], axis=0)
    lane = iota(pieces.shape, 1)
    on_both = jnp.where(lane < wide, pieces, pltpu.roll(pieces, wide, 1))[:, : 2 * wide].astype(BF16)
    pieces = pltpu.roll(pieces, LANES - wide, 1)
    on_w = jnp.where(lane < COLS, pieces, pltpu.roll(pieces, COLS, 1))[:, : 2 * COLS].astype(BF16)
    group = size_x // 8
    for x in range(size_x):
        at = slice(x * SUB * LANES, (x + 1) * SUB * LANES)
        block = plain_dot(on_both, both_ref[:, at]) + plain_dot(on_w, w_ref[:, at])
        block = block[:COLS] + block[COLS:]
        for y in range(SUB):
            result[x * SUB + y] = block[:, y * LANES : (y + 1) * LANES]
        if x % group == group - 1:
            for c in range(COLS):
                copies.append(pltpu.make_async_copy(
                    result.at[pl.ds((x + 1 - group) * SUB, group * SUB), c],
                    next_ref.at[c, pl.ds((x + 1 - group) * SUB, group * SUB)],
                    sems.at[x // group, c],
                ))
                copies[-1].start()
    for copy in copies:
        copy.wait()


def swaps(devices):
    first = [(i, i ^ 1) for i in range(devices)]
    second = [pair for i in range(1, devices - 1, 2) for pair in ((i, i + 1), (i + 1, i))]
    return first, second


def per_device(basis, classes, ports, taps, port_gain):
    size_x, size_y, size_z = classes.shape
    x_first, x_second = swaps(lax.axis_size(GX))
    y_first, y_second = swaps(lax.axis_size(GY))
    shape = jax.ShapeDtypeStruct
    wide, cells, lines = BLOCKS * COLS, size_x * size_y * size_z, size_x * SUB
    tile = shape((SUB, LANES), F32)
    edge = shape((COLS, REACH, SUB, LANES), F32)
    block, xa, xb = pl.pallas_call(
        edges_kernel,
        out_shape=(shape((COLS, size_x, SUB, LANES), F32), edge, edge),
        in_specs=[HBM],
        out_specs=(VMEM,) * 3,
        scratch_shapes=[pltpu.SemaphoreType.DMA((3,))],
        compiler_params=limit(4),
        name="edges",
    )(in_hbm(basis))
    yb = lax.ppermute(block, GY, y_second)
    xb = lax.ppermute(xb, GX, x_second)
    xa = lax.ppermute(xa, GX, x_first)
    ya = lax.ppermute(block, GY, y_first)
    part, coef_x, coef_y, both, sums = pl.pallas_call(
        local_kernel,
        out_shape=(
            shape((size_x, COLS, SUB, LANES), F32),
            shape((size_x, REACH, SUB, LANES), F32),
            shape((size_x, REACH, SUB, LANES), F32),
            shape((2 * wide, cells), BF16),
            tile,
        ),
        in_specs=[VMEM, VMEM, HBM, VMEM, HBM, HBM],
        out_specs=(VMEM,) * 5,
        scratch_shapes=[
            pltpu.VMEM((size_x + 2 * REACH, COLS, SUB, LANES), F32),
            pltpu.VMEM((size_x, COLS, 2 * SUB, LANES), F32),
            pltpu.VMEM((PORTS, SUB, LANES), F32),
            pltpu.VMEM((SUB, LANES), F32),
            pltpu.VMEM(((6 * REACH + 1) * SUB, 3 * MAT * SUB), BF16),
            pltpu.VMEM(((6 * REACH + 1) * SUB, LANES), F32),
            pltpu.VMEM((lines, wide, LANES), F32),
            pltpu.VMEM((size_x, SUB, LANES), jnp.int32),
            pltpu.VMEM((size_x, SUB, LANES), jnp.int32),
            pltpu.SemaphoreType.DMA((2 + wide,)),
        ],
        compiler_params=limit(16),
        cost_estimate=pl.CostEstimate(flops=10**9, bytes_accessed=8 * 2**20, transcendentals=0),
        name="local",
    )(taps, port_gain[None], in_hbm(basis.reshape(wide, lines, LANES)), block, in_hbm(classes), in_hbm(ports))
    w, sums = pl.pallas_call(
        halo_kernel,
        out_shape=(shape((2 * COLS, cells), BF16), tile),
        in_specs=[VMEM] * 9,
        out_specs=(VMEM,) * 2,
        scratch_shapes=[
            pltpu.VMEM((size_x, COLS, 2 * SUB, LANES), F32),
            pltpu.VMEM((2 * REACH, COLS, SUB, LANES), F32),
            pltpu.VMEM((2 * COLS, LANES), F32),
        ],
        compiler_params=limit(8),
        name="halo",
    )(part, coef_x, coef_y, both, sums, xa, xb, ya, yb)

    def fold(copies, *tiles):
        return pl.pallas_call(
            fold_kernel,
            out_shape=shape((copies, SUB, LANES), F32),
            in_specs=[VMEM] * len(tiles),
            out_specs=VMEM,
            compiler_params=limit(2),
            name="fold",
        )(*tiles)

    beside = lax.ppermute(sums, "gy_1", [(0, 1), (1, 0)])
    along_gx = lax.all_to_all(fold(lax.axis_size(GX), sums, beside), GX, 0, 0)
    received = lax.all_to_all(fold(lax.axis_size("gy_0"), along_gx), "gy_0", 0, 0)
    total = cells * lax.axis_size(GX) * lax.axis_size(GY)
    next_block, projection, triangle = pl.pallas_call(
        functools.partial(finish_kernel, 1.0 / total),
        out_shape=(
            shape((COLS, lines, LANES), F32),
            shape((COLS, wide), F32),
            shape((COLS, COLS), F32),
        ),
        in_specs=[VMEM] * 4,
        out_specs=(HBM, HBM, HBM),
        scratch_shapes=[
            pltpu.VMEM((MAT, LANES), F32),
            pltpu.VMEM((lines, COLS, LANES), F32),
            pltpu.SemaphoreType.DMA((8, COLS)),
            pltpu.VMEM((COLS, wide), F32),
            pltpu.VMEM((COLS, COLS), F32),
            pltpu.SemaphoreType.DMA((2,)),
        ],
        compiler_params=limit(8),
        name="finish",
    )(taps, received, both, w)
    return next_block.reshape(COLS, size_x, size_y, size_z), projection.T, triangle


def solution(mesh):
    split_mesh = Mesh(mesh.devices.reshape(4, 8, 16, 2), AXES)
    in_specs = (P(None, GX, GY, None), P(GX, GY, None), P(GX, GY, None), P(), P())
    out_specs = (P(None, GX, GY, None), P(), P())
    return jax.shard_map(
        per_device, mesh=split_mesh, in_specs=in_specs, out_specs=out_specs, check_vma=False
    )
```
